32 devices in a mesh: groups: 2 (over y), members: 4 (over z), segment: 2 (over x), rows: 2 (over core).
Axes of the slice: x: 2, y: 2, z: 4, core: 2. Of those that a mesh axis runs over, the one named last changes fastest.
Arguments:
- init_state: bfloat16 [4, 2, 77, 128], P(('groups', 'segment'), 'rows'), parts along dimension 0, may hold values from -6 to 6
- forcing_slots: bfloat16 [4, 4, 2, 2, 4, 128], P('members', ('groups', 'segment'), None, 'rows'), parts along dimension 1, may hold values from -6 to 6
- atmos_owner: int32 [4, 2], P(('groups', 'segment')), parts along dimension 0, may hold values from 0 to 3
- land_mask: int32 [4, 128], P(('groups', 'rows')), parts along dimension 0, may hold values 0 or 1
- param_index: int32 [8], P(('groups', 'members')), parts along dimension 0, may hold values from 0 to 63
- settings: float32 [64, 16], replicated, may hold values from -5 to 5
- scale_weight: float32 [16, 256], replicated, may hold values from -0.75 to 0.75
- shift_weight: float32 [16, 256], replicated, may hold values from -0.75 to 0.75
- encode_weight: bfloat16 [256, 81], replicated, may hold values from -0.625 to 0.625
- conv_weight: bfloat16 [2, 256, 2304], P('segment'), may hold values from -0.125 to 0.125
- point_weight: bfloat16 [2, 256, 256], P('segment'), may hold values from -0.375 to 0.375
- norm_gain: bfloat16 [2, 256], P('segment'), may hold values from 0.099609375 to 1.8984375
- decode_weight: bfloat16 [77, 256], replicated, may hold values from -0.1875 to 0.1875
Outputs:
- final_state: bfloat16 [4, 4, 2, 77, 128], P('members', ('groups', 'segment'), 'rows'), parts along dimension 1
- ensemble_mean: float32 [4, 2, 77, 128], P(('groups', 'segment'), 'rows'), parts along dimension 0
The draws below stay inside these ranges and needn't reach their ends.
There are 2 independent parts, one for each index of `groups`. The reference program is written for one: setup_inputs(seed, part) draws one part's arguments, and reference() takes and returns one part's arrays. A program takes and returns all parts, laid end to end along the dimension named above; an argument that names none is the same for every part. Nothing has to cross between parts.
Inputs may be any that keep to these rules, and one draw needn't show every extreme that they name: `atmos_owner`: a member index of the same group. `param_index`: a row of settings.
All inputs are finite; a program needn't handle non-finite values. No bound on the sum of `land_mask` on one device may be relied on, other than what follows from the above.
Results may differ from the reference program's by a relative error of at most 0.018.
Values may be sent and summed in bfloat16 or wider, within the bound.
A program may use at most 64 MiB of HBM per device.

```python
import jax
import jax.numpy as jnp
from jax import lax

C = 256
V = 77
F = 4
P_SIZE = 16
NSET = 64
STEPS = 2
LON_DEV = 128
LAYERS = 2
DATES = 2
MEMBERS = 4
LAT = 2


def touch_ends(values, own_key, least, top_value):
    extent = values.shape
    index_at = [jax.random.randint(jax.random.fold_in(own_key, axis), (), 0, extent[axis]) for axis in range(len(extent))]
    values = values.at[tuple(index_at)].set(least)
    longest = extent.index(max(extent))
    index_at[longest] = (index_at[longest] + 1) % extent[longest]
    return values.at[tuple(index_at)].set(top_value)


def levels(stream_key, extent, cuts, low, largest):
    def one(axis_at, parts):
        steps = jax.random.uniform(jax.random.fold_in(jax.random.fold_in(stream_key, 6), axis_at), (parts,), jnp.float32, low / len(cuts), largest / len(cuts))
        return jnp.repeat(jnp.exp(steps), extent[axis_at] // parts).reshape((-1,) + (1,) * (len(extent) - axis_at - 1))

    level = one(*cuts[0])
    for cut in cuts[1:]:
        level = level * one(*cut)
    return level


def scatter_about(own_key, shape, deviation, limit, cuts=(), kind=jnp.bfloat16):
    loudness = levels(own_key, shape, cuts, -0.22, 0.18) if cuts else 1.0
    drawn = jax.random.normal(own_key, shape, jnp.float32) * deviation * loudness
    return jnp.minimum(jnp.maximum(drawn, -limit), limit).astype(kind)


def setup_inputs(seed: int = 0, part: int = 0) -> dict:
    seeds = jax.random.split(jax.random.key(seed), 14)
    part_keys = jax.random.split(jax.random.fold_in(seeds[13], part), 14)
    init_state = scatter_about(part_keys[0], (DATES, LAT, V, LON_DEV), 1.0, 6.0, ((0, 2), (1, 2)))
    forcing_slots = scatter_about(part_keys[1], (MEMBERS, DATES, STEPS, LAT, F, LON_DEV), 1.0, 6.0, ((0, 4), (1, 2), (3, 2)))
    atmos_owner = touch_ends(jax.random.randint(part_keys[2], (DATES, STEPS), 0, MEMBERS), jax.random.fold_in(part_keys[2], 1), 0, MEMBERS - 1).astype(jnp.int32)
    land_mask = touch_ends((jax.random.randint(part_keys[3], (LAT, LON_DEV), 0, 4) < 3).astype(jnp.int32), jax.random.fold_in(part_keys[3], 1), 0, 1)
    param_index = touch_ends(jax.random.randint(part_keys[4], (MEMBERS,), 0, NSET), jax.random.fold_in(part_keys[4], 1), 0, NSET - 1).astype(jnp.int32)
    settings = scatter_about(seeds[5], (NSET, P_SIZE), 1.0, 5.0, (), jnp.float32)
    scale_weight = scatter_about(seeds[6], (P_SIZE, C), (4 * P_SIZE) ** -0.5, 0.75, (), jnp.float32)
    shift_weight = scatter_about(seeds[7], (P_SIZE, C), (4 * P_SIZE) ** -0.5, 0.75, (), jnp.float32)
    encode_weight = scatter_about(seeds[8], (C, V + F), (V + F) ** -0.5, 0.625)
    conv_weight = scatter_about(seeds[9], (LAYERS, C, 9 * C), (9 * C) ** -0.5, 0.125, ((0, 2),))
    point_weight = scatter_about(seeds[10], (LAYERS, C, C), C ** -0.5, 0.375, ((0, 2),))
    norm_gain = jnp.clip(1.0 + 0.18 * jax.random.normal(seeds[11], (LAYERS, C), jnp.float32), 0.099609375, 1.8984375).astype(jnp.bfloat16)
    decode_weight = scatter_about(seeds[12], (V, C), (4 * C) ** -0.5, 0.1875)
    return dict(init_state=init_state, forcing_slots=forcing_slots, atmos_owner=atmos_owner, land_mask=land_mask, param_index=param_index, settings=settings, scale_weight=scale_weight, shift_weight=shift_weight, encode_weight=encode_weight, conv_weight=conv_weight, point_weight=point_weight, norm_gain=norm_gain, decode_weight=decode_weight)


def lat_lon_taps(field, spacing):
    lat_cells = field.shape[-3]
    lon_cells = field.shape[-1]
    padded = jnp.pad(field, [(0, 0)] * (field.ndim - 3) + [(1, 1), (0, 0), (4, 4)])
    pieces = []
    for lat_off in range(3):
        lat_band = padded[..., lat_off:lat_off + lat_cells, :, :]
        for lon_off in (-1, 0, 1):
            begin = 4 + lon_off * spacing
            pieces.append(lat_band[..., begin:begin + lon_cells])
    return jnp.concatenate(pieces, axis=-2)

def section(hidden, conv_here, point_here, gain_here, spacing, land_cells):
    taps = lat_lon_taps(hidden, spacing).astype(jnp.float32)
    conv_out = jnp.einsum('ok,dlkx->dlox', conv_here.astype(jnp.float32), taps)
    chan_mean = lax.optimization_barrier(jnp.mean(conv_out, axis=-2, keepdims=True))
    centred = conv_out - chan_mean
    spread = lax.optimization_barrier(jnp.mean(centred * centred, axis=-2, keepdims=True))
    normed = centred * lax.rsqrt(spread + 1e-05) * gain_here.astype(jnp.float32)[:, None]
    activated = jax.nn.gelu(normed).astype(jnp.bfloat16)
    mixed = jnp.einsum('ok,dlkx->dlox', point_here.astype(jnp.float32), activated.astype(jnp.float32))
    return (land_cells * (hidden.astype(jnp.float32) + mixed)).astype(jnp.bfloat16)

def reference(init_state, forcing_slots, atmos_owner, land_mask, param_index, settings, scale_weight, shift_weight, encode_weight, conv_weight, point_weight, norm_gain, decode_weight):
    land_cells = land_mask.astype(jnp.float32)[:, None, :]
    date_ids = jnp.arange(DATES)
    per_step = []
    for step_no in range(STEPS):
        per_step.append(forcing_slots[atmos_owner[:, step_no], date_ids, step_no])
    forcing = jnp.stack(per_step, axis=1)

    def run_member(member_row):
        setting_row = settings[member_row]
        cond_scale = 1.0 + jnp.dot(setting_row, scale_weight, precision=lax.Precision.HIGHEST)
        cond_shift = jnp.dot(setting_row, shift_weight, precision=lax.Precision.HIGHEST)
        ocean_state = init_state
        for step_no in range(STEPS):
            inputs = jnp.concatenate([ocean_state, forcing[:, step_no]], axis=2).astype(jnp.float32)
            lifted = jnp.einsum('ok,dlkx->dlox', encode_weight.astype(jnp.float32), inputs)
            hidden = (land_cells * (lifted * cond_scale[:, None] + cond_shift[:, None])).astype(jnp.bfloat16)
            for layer in range(LAYERS):
                hidden = section(hidden, conv_weight[layer], point_weight[layer], norm_gain[layer], 2 ** (layer % 3), land_cells)
            change = jnp.einsum('ok,dlkx->dlox', decode_weight.astype(jnp.float32), hidden.astype(jnp.float32))
            ocean_state = (ocean_state.astype(jnp.float32) + land_cells * change).astype(jnp.bfloat16)
        return ocean_state
    finals = lax.map(run_member, param_index)
    return (finals, lax.optimization_barrier(jnp.mean(finals.astype(jnp.float32), axis=0)))
```

```python
import functools

import jax
import jax.numpy as jnp
from jax import lax
from jax.experimental import pallas as pl
from jax.experimental.pallas import tpu as pltpu
from jax.sharding import PartitionSpec as P

STEPS = 2
CONV_CHUNKS = 4
MESH = pl.DeviceIdType.MESH


def to_column(row):
    size = row.shape[1]
    at = lax.broadcasted_iota(jnp.int32, (size, size), 0)
    along = lax.broadcasted_iota(jnp.int32, (size, size), 1)
    return jnp.sum(jnp.where(at == along, row, 0.0), axis=1, keepdims=True)


def shifted(field, offset):
    if offset == 0:
        return field
    lon = field.shape[1]
    place = lax.broadcasted_iota(jnp.int32, field.shape, 1)
    moved = pltpu.roll(field, (-offset) % lon, 1)
    return jnp.where((place + offset >= 0) & (place + offset < lon), moved, 0.0)


def kernel(
    sizes,
    init_ref,
    slots_ref,
    owner_ref,
    land_ref,
    param_ref,
    settings_ref,
    scale_ref,
    shift_ref,
    encode_ref,
    conv_ref,
    point_ref,
    gain_ref,
    decode_ref,
    final_ref,
    mean_ref,
    conv_all,
    point_all,
    gain_all,
    init_other,
    land_other,
    force_all,
    final_all,
    inputs,
    taps,
    pair_send,
    pair_recv,
    force_send,
    force_recv,
    seg_send,
    seg_recv,
    grp_send,
    grp_recv,
    core_send,
    core_recv,
    gain_send,
    gain_recv,
    mean_send,
    mean_recv,
    own_sem,
):
    groups, members, segments, rows = sizes
    g = lax.axis_index("groups")
    m = lax.axis_index("members")
    s = lax.axis_index("segment")
    r = lax.axis_index("rows")
    channels = conv_all.shape[1]
    lon = init_ref.shape[3]

    def ahead(value, step, size):
        return lax.rem(value + step, size)

    def device(dg=0, dm=0, ds=0, dr=0):
        return (
            ahead(g, dg, groups),
            ahead(m, dm, members),
            ahead(s, ds, segments),
            ahead(r, dr, rows),
        )

    mates = [(dm, dr) for dm in range(members) for dr in range(rows) if dm or dr]
    barrier = pltpu.get_barrier_semaphore()
    met = 0
    for dm, dr in mates:
        pl.semaphore_signal(barrier, inc=1, device_id=device(dm=dm, dr=dr), device_id_type=MESH)
        met += 1
    for ds in range(1, segments):
        pl.semaphore_signal(barrier, inc=1, device_id=device(ds=ds), device_id_type=MESH)
        met += 1
    for dg in range(1, groups):
        pl.semaphore_signal(barrier, inc=1, device_id=device(dg=dg), device_id_type=MESH)
        met += 1
    pl.semaphore_wait(barrier, met)

    def send(source, target, send_sem, recv_sem, to):
        return pltpu.make_async_remote_copy(
            src_ref=source,
            dst_ref=target,
            send_sem=send_sem,
            recv_sem=recv_sem,
            device_id=to,
            device_id_type=MESH,
        )

    share = channels // (groups * rows)
    chunk = share // CONV_CHUNKS

    def piece(group, row, index):
        start = (group * rows + row) * share
        if index < CONV_CHUNKS:
            return pl.ds(pl.multiple_of(start + index * chunk, chunk), chunk)
        return pl.ds(pl.multiple_of(start, share), share)

    def view(layer, group, row, index):
        part = conv_all if index < CONV_CHUNKS else point_all
        return part.at[layer, piece(group, row, index)]

    def source_view(index):
        part = conv_ref if index < CONV_CHUNKS else point_ref
        return part.at[0, piece(g, r, index)]

    pieces = range(CONV_CHUNKS + 1)
    seg_copies = {}
    for index in pieces:
        for ds in range(1, segments):
            copy = send(
                source_view(index),
                view(s, g, r, index),
                seg_send.at[ds - 1, index],
                seg_recv.at[ds - 1, index],
                device(ds=ds),
            )
            copy.start()
            seg_copies[ds, index] = copy
    others = []
    other_row = device(dr=1)
    init_copy = send(init_ref.at[0, 0], init_other, pair_send.at[0], pair_recv.at[0], other_row)
    land_copy = send(land_ref, land_other, pair_send.at[1], pair_recv.at[1], other_row)
    others += [init_copy, land_copy]
    for index, (dm, dr) in enumerate(mates):
        others.append(
            send(
                slots_ref.at[0, 0, :, 0],
                force_all.at[m, r],
                force_send.at[index],
                force_recv.at[index],
                device(dm=dm, dr=dr),
            )
        )
    for ds in range(1, segments):
        others.append(
            send(gain_ref, gain_all.at[s], gain_send.at[ds - 1], gain_recv.at[ds - 1], device(ds=ds))
        )
    for copy in others:
        copy.start()
    own = [
        pltpu.make_async_copy(conv_ref.at[0], conv_all.at[s], own_sem.at[0]),
        pltpu.make_async_copy(point_ref.at[0], point_all.at[s], own_sem.at[1]),
        pltpu.make_async_copy(gain_ref, gain_all.at[s], own_sem.at[2]),
        pltpu.make_async_copy(slots_ref.at[0, 0, :, 0], force_all.at[m, r], own_sem.at[3]),
    ]
    for copy in own:
        copy.start()

    chosen = lax.broadcasted_iota(jnp.int32, settings_ref.shape, 0) == param_ref[0]
    setting_row = jnp.sum(jnp.where(chosen, settings_ref[...], 0.0), axis=0, keepdims=True)
    setting = to_column(setting_row)
    cond_scale = to_column(1.0 + jnp.sum(setting * scale_ref[...], axis=0, keepdims=True))
    cond_shift = to_column(jnp.sum(setting * shift_ref[...], axis=0, keepdims=True))
    encode_weight = encode_ref[...]
    decode_weight = decode_ref[...]
    for copy in others:
        copy.wait()
    for copy in own:
        copy.wait()

    head = r == 0
    mine, theirs = init_ref[0, 0].astype(jnp.float32), init_other[...].astype(jnp.float32)
    state = jnp.concatenate(
        [jnp.where(head, mine, theirs), jnp.where(head, theirs, mine)], axis=1
    )
    land_mine = land_ref[...].astype(jnp.float32)
    land_theirs = land_other[...].astype(jnp.float32)
    land = jnp.concatenate(
        [jnp.where(head, land_mine, land_theirs), jnp.where(head, land_theirs, land_mine)], axis=1
    )
    variables = state.shape[0]
    forces = slots_ref.shape[4]

    def encoded(state, step_no):
        owner = owner_ref[0, step_no]
        inputs[0:variables, :] = state
        for row in range(rows):
            total = jnp.zeros((forces, lon), jnp.float32)
            for member in range(members):
                slot = force_all[member, row, step_no].astype(jnp.float32)
                total = total + jnp.where(owner == member, slot, 0.0)
            inputs[variables : variables + forces, row * lon : (row + 1) * lon] = total
        fields = inputs[...][: variables + forces].astype(jnp.bfloat16)
        lifted = jnp.dot(encode_weight, fields, preferred_element_type=jnp.float32)
        return (land * (lifted * cond_scale + cond_shift)).astype(jnp.bfloat16)

    hidden = encoded(state, 0)

    relays = []
    for index in pieces:
        for ds in range(1, segments):
            layer = lax.rem(s - ds + segments, segments)
            seg_copies[ds, index].wait_recv()
            here = view(layer, g, r, index)
            grp = {}
            for dg in range(1, groups):
                copy = send(
                    here,
                    here,
                    grp_send.at[ds - 1, dg - 1, index],
                    grp_recv.at[ds - 1, dg - 1, index],
                    device(dg=dg),
                )
                copy.start()
                grp[dg] = copy
            copy = send(
                here,
                here,
                core_send.at[ds - 1, 0, index],
                core_recv.at[ds - 1, 0, index],
                other_row,
            )
            copy.start()
            relays.append((layer, ds, index, grp, copy))
    waits = []
    for layer, ds, index, grp, copy in relays:
        waits.append(copy)
        for dg in range(1, groups):
            grp[dg].wait_recv()
            there = view(layer, lax.rem(g - dg + groups, groups), r, index)
            relay = send(
                there,
                there,
                core_send.at[ds - 1, dg, index],
                core_recv.at[ds - 1, dg, index],
                other_row,
            )
            relay.start()
            waits.append(relay)
    for copy in waits:
        copy.wait_recv()

    for step_no in range(STEPS):
        if step_no:
            hidden = encoded(state, step_no)
        for layer in range(segments):
            spacing = 2 ** (layer % 3)
            wide = hidden.astype(jnp.float32)
            for row in range(rows):
                here = wide[:, row * lon : (row + 1) * lon]
                for at, offset in enumerate((-spacing, 0, spacing)):
                    taps[at * channels : (at + 1) * channels, row * lon : (row + 1) * lon] = shifted(
                        here, offset
                    ).astype(jnp.bfloat16)
            span = 3 * channels
            conv = jnp.dot(
                conv_all[layer, :, span : 2 * span], taps[...], preferred_element_type=jnp.float32
            )
            below = jnp.dot(
                conv_all[layer, :, 2 * span :], taps[:, lon:], preferred_element_type=jnp.float32
            )
            above = jnp.dot(
                conv_all[layer, :, :span], taps[:, :lon], preferred_element_type=jnp.float32
            )
            conv = conv + jnp.concatenate([below, above], axis=1)
            centred = conv - jnp.mean(conv, axis=0, keepdims=True)
            spread = jnp.mean(centred * centred, axis=0, keepdims=True)
            gain = to_column(gain_all[layer].astype(jnp.float32))
            normed = centred * lax.rsqrt(spread + 1e-05) * gain
            activated = jax.nn.gelu(normed).astype(jnp.bfloat16)
            mixed = jnp.dot(point_all[layer], activated, preferred_element_type=jnp.float32)
            hidden = (land * (wide + mixed)).astype(jnp.bfloat16)
        change = jnp.dot(decode_weight, hidden, preferred_element_type=jnp.float32)
        state = (state + land * change).astype(jnp.bfloat16).astype(jnp.float32)

    own_final = jnp.where(head, state[:, :lon], state[:, lon:])
    final_ref[0, 0, 0] = own_final.astype(jnp.bfloat16)
    mean_copies = []
    for dm in range(1, members):
        copy = send(
            final_ref.at[0, 0, 0],
            final_all.at[m],
            mean_send.at[dm - 1],
            mean_recv.at[dm - 1],
            device(dm=dm),
        )
        copy.start()
        mean_copies.append(copy)
    final_all[m] = own_final.astype(jnp.bfloat16)
    for copy in seg_copies.values():
        copy.wait_send()
    for layer, ds, index, grp, copy in relays:
        for dg in range(1, groups):
            grp[dg].wait_send()
    for copy in waits:
        copy.wait_send()
    for copy in mean_copies:
        copy.wait()
    total = jnp.zeros(own_final.shape, jnp.float32)
    for member in range(members):
        total = total + final_all[member].astype(jnp.float32)
    mean_ref[0, 0] = total / members


def solution(mesh):
    sizes = tuple(mesh.shape[axis] for axis in ("groups", "members", "segment", "rows"))
    groups, members, segments, rows = sizes

    def per_device(*args):
        init, slots, conv = args[0], args[1], args[9]
        variables, lon = init.shape[2:]
        forces = slots.shape[4]
        channels = conv.shape[1]
        vmem = pl.BlockSpec(memory_space=pltpu.VMEM)
        smem = pl.BlockSpec(memory_space=pltpu.SMEM)
        hbm = pl.BlockSpec(memory_space=pl.ANY)
        in_specs = [vmem] * 13
        in_specs[2] = in_specs[4] = smem
        in_specs[9] = in_specs[10] = hbm
        dma = pltpu.SemaphoreType.DMA
        pieces = CONV_CHUNKS + 1
        mates = members * rows - 1
        away = max(segments - 1, 1)
        scratch = [
            pltpu.VMEM((segments,) + conv.shape[1:], jnp.bfloat16),
            pltpu.VMEM((segments, channels, channels), jnp.bfloat16),
            pltpu.VMEM((segments, 1, channels), jnp.bfloat16),
            pltpu.VMEM((variables, lon), jnp.bfloat16),
            pltpu.VMEM((1, lon), jnp.int32),
            pltpu.VMEM((members, rows, STEPS, forces, lon), jnp.bfloat16),
            pltpu.VMEM((members, variables, lon), jnp.bfloat16),
            pltpu.VMEM((-(-(variables + forces) // 8) * 8, rows * lon), jnp.float32),
            pltpu.VMEM((3 * channels, rows * lon), jnp.bfloat16),
            dma((2,)),
            dma((2,)),
            dma((mates,)),
            dma((mates,)),
            dma((away, pieces)),
            dma((away, pieces)),
            dma((away, max(groups - 1, 1), pieces)),
            dma((away, max(groups - 1, 1), pieces)),
            dma((away, groups, pieces)),
            dma((away, groups, pieces)),
            dma((away,)),
            dma((away,)),
            dma((max(members - 1, 1),)),
            dma((max(members - 1, 1),)),
            dma((4,)),
        ]
        return pl.pallas_call(
            functools.partial(kernel, sizes),
            out_shape=(
                jax.ShapeDtypeStruct((1, 1, 1, variables, lon), jnp.bfloat16),
                jax.ShapeDtypeStruct((1, 1, variables, lon), jnp.float32),
            ),
            in_specs=in_specs,
            out_specs=(vmem, vmem),
            scratch_shapes=scratch,
            compiler_params=pltpu.CompilerParams(
                collective_id=0, has_side_effects=True, vmem_limit_bytes=48 * 1024 * 1024
            ),
        )(*args)

    in_specs = (
        P(("groups", "segment"), "rows", None, None),
        P("members", ("groups", "segment"), None, "rows", None, None),
        P(("groups", "segment"), None),
        P(("groups", "rows"), None),
        P(("groups", "members")),
        P(),
        P(),
        P(),
        P(),
        P("segment", None, None),
        P("segment", None, None),
        P("segment", None),
        P(),
    )
    out_specs = (
        P("members", ("groups", "segment"), "rows", None, None),
        P(("groups", "segment"), "rows", None, None),
    )
    return jax.shard_map(
        per_device, mesh=mesh, in_specs=in_specs, out_specs=out_specs, check_vma=False
    )
```

```python
import functools

import jax
import jax.numpy as jnp
from jax import lax
from jax.experimental import pallas as pl
from jax.experimental.pallas import tpu as pltpu
from jax.sharding import PartitionSpec as P

STEPS = 2
CONV_CHUNKS = 4
MESH = pl.DeviceIdType.MESH


def to_column(row):
    size = row.shape[1]
    at = lax.broadcasted_iota(jnp.int32, (size, size), 0)
    along = lax.broadcasted_iota(jnp.int32, (size, size), 1)
    return jnp.sum(jnp.where(at == along, row, 0.0), axis=1, keepdims=True)


def shifted(field, offset):
    if offset == 0:
        return field
    lon = field.shape[1]
    place = lax.broadcasted_iota(jnp.int32, field.shape, 1)
    moved = pltpu.roll(field, (-offset) % lon, 1)
    return jnp.where((place + offset >= 0) & (place + offset < lon), moved, 0.0)


def kernel(
    sizes,
    init_hbm,
    slots_ref,
    owner_hbm,
    land_hbm,
    param_hbm,
    settings_hbm,
    scale_hbm,
    shift_hbm,
    encode_hbm,
    conv_ref,
    point_ref,
    gain_ref,
    decode_hbm,
    final_ref,
    mean_ref,
    init_ref,
    owner_ref,
    land_ref,
    param_ref,
    settings_ref,
    scale_ref,
    shift_ref,
    encode_ref,
    decode_ref,
    conv_all,
    point_all,
    gain_all,
    init_other,
    land_other,
    force_all,
    final_all,
    inputs,
    taps,
    pair_send,
    pair_recv,
    force_send,
    force_recv,
    seg_send,
    seg_recv,
    grp_send,
    grp_recv,
    core_send,
    core_recv,
    gain_send,
    gain_recv,
    mean_send,
    mean_recv,
    own_sem,
):
    groups, members, segments, rows = sizes
    g = lax.axis_index("groups")
    m = lax.axis_index("members")
    s = lax.axis_index("segment")
    r = lax.axis_index("rows")
    channels = conv_all.shape[1]
    lon = init_hbm.shape[3]

    def ahead(value, step, size):
        return lax.rem(value + step, size)

    def device(dg=0, dm=0, ds=0, dr=0):
        return (
            ahead(g, dg, groups),
            ahead(m, dm, members),
            ahead(s, ds, segments),
            ahead(r, dr, rows),
        )

    fetched = [
        (owner_hbm, owner_ref),
        (param_hbm, param_ref),
        (settings_hbm, settings_ref),
        (scale_hbm, scale_ref),
        (shift_hbm, shift_ref),
        (encode_hbm, encode_ref),
        (init_hbm, init_ref),
        (land_hbm, land_ref),
        (decode_hbm, decode_ref),
        (gain_ref, gain_all.at[s]),
        (slots_ref.at[0, 0, :, 0], force_all.at[m, r]),
        (conv_ref.at[0], conv_all.at[s]),
        (point_ref.at[0], point_all.at[s]),
    ]
    own = []
    for index, (source, target) in enumerate(fetched):
        copy = pltpu.make_async_copy(source, target, own_sem.at[index])
        copy.start()
        own.append(copy)

    mates = [(dm, dr) for dm in range(members) for dr in range(rows) if dm or dr]
    barrier = pltpu.get_barrier_semaphore()
    met = 0
    for dm, dr in mates:
        pl.semaphore_signal(barrier, inc=1, device_id=device(dm=dm, dr=dr), device_id_type=MESH)
        met += 1
    for ds in range(1, segments):
        pl.semaphore_signal(barrier, inc=1, device_id=device(ds=ds), device_id_type=MESH)
        met += 1
    for dg in range(1, groups):
        pl.semaphore_signal(barrier, inc=1, device_id=device(dg=dg), device_id_type=MESH)
        met += 1
    pl.semaphore_wait(barrier, met)

    def send(source, target, send_sem, recv_sem, to):
        return pltpu.make_async_remote_copy(
            src_ref=source,
            dst_ref=target,
            send_sem=send_sem,
            recv_sem=recv_sem,
            device_id=to,
            device_id_type=MESH,
        )

    share = channels // (groups * rows)
    chunk = share // CONV_CHUNKS

    def piece(group, row, index):
        start = (group * rows + row) * share
        if index < CONV_CHUNKS:
            return pl.ds(pl.multiple_of(start + index * chunk, chunk), chunk)
        return pl.ds(pl.multiple_of(start, share), share)

    def view(layer, group, row, index):
        part = conv_all if index < CONV_CHUNKS else point_all
        return part.at[layer, piece(group, row, index)]

    def source_view(index):
        part = conv_ref if index < CONV_CHUNKS else point_ref
        return part.at[0, piece(g, r, index)]

    pieces = range(CONV_CHUNKS + 1)
    seg_copies = {}
    for index in pieces:
        for ds in range(1, segments):
            copy = send(
                source_view(index),
                view(s, g, r, index),
                seg_send.at[ds - 1, index],
                seg_recv.at[ds - 1, index],
                device(ds=ds),
            )
            copy.start()
            seg_copies[ds, index] = copy
    others = []
    other_row = device(dr=1)
    init_copy = send(init_hbm.at[0, 0], init_other, pair_send.at[0], pair_recv.at[0], other_row)
    land_copy = send(land_hbm, land_other, pair_send.at[1], pair_recv.at[1], other_row)
    others += [init_copy, land_copy]
    for index, (dm, dr) in enumerate(mates):
        others.append(
            send(
                slots_ref.at[0, 0, :, 0],
                force_all.at[m, r],
                force_send.at[index],
                force_recv.at[index],
                device(dm=dm, dr=dr),
            )
        )
    for ds in range(1, segments):
        others.append(
            send(gain_ref, gain_all.at[s], gain_send.at[ds - 1], gain_recv.at[ds - 1], device(ds=ds))
        )
    for copy in others:
        copy.start()
    for copy in own:
        copy.wait()
    chosen = lax.broadcasted_iota(jnp.int32, settings_ref.shape, 1) == param_ref[0]
    setting = jnp.sum(jnp.where(chosen, settings_ref[...], 0.0), axis=1, keepdims=True)
    cond_scale = to_column(1.0 + jnp.sum(setting * scale_ref[...], axis=0, keepdims=True))
    cond_shift = to_column(jnp.sum(setting * shift_ref[...], axis=0, keepdims=True))
    encode_weight = encode_ref[...]
    decode_weight = decode_ref[...]
    for copy in others:
        copy.wait()

    head = r == 0
    mine, theirs = init_ref[0, 0].astype(jnp.float32), init_other[...].astype(jnp.float32)
    state = jnp.concatenate(
        [jnp.where(head, mine, theirs), jnp.where(head, theirs, mine)], axis=1
    )
    land_mine = land_ref[...].astype(jnp.float32)
    land_theirs = land_other[...].astype(jnp.float32)
    land = jnp.concatenate(
        [jnp.where(head, land_mine, land_theirs), jnp.where(head, land_theirs, land_mine)], axis=1
    )
    variables = state.shape[0]
    forces = slots_ref.shape[4]

    def encoded(state, step_no):
        owner = owner_ref[0, step_no]
        inputs[0:variables, :] = state
        for row in range(rows):
            total = jnp.zeros((forces, lon), jnp.float32)
            for member in range(members):
                slot = force_all[member, row, step_no].astype(jnp.float32)
                total = total + jnp.where(owner == member, slot, 0.0)
            inputs[variables : variables + forces, row * lon : (row + 1) * lon] = total
        fields = inputs[...][: variables + forces].astype(jnp.bfloat16)
        lifted = lax.dot_general(
            encode_weight, fields, (((0,), (0,)), ((), ())), preferred_element_type=jnp.float32
        )
        return (land * (lifted * cond_scale + cond_shift)).astype(jnp.bfloat16)

    hidden = encoded(state, 0)

    relays = []
    for index in pieces:
        for ds in range(1, segments):
            layer = lax.rem(s - ds + segments, segments)
            seg_copies[ds, index].wait_recv()
            here = view(layer, g, r, index)
            grp = {}
            for dg in range(1, groups):
                copy = send(
                    here,
                    here,
                    grp_send.at[ds - 1, dg - 1, index],
                    grp_recv.at[ds - 1, dg - 1, index],
                    device(dg=dg),
                )
                copy.start()
                grp[dg] = copy
            copy = send(
                here,
                here,
                core_send.at[ds - 1, 0, index],
                core_recv.at[ds - 1, 0, index],
                other_row,
            )
            copy.start()
            relays.append((layer, ds, index, grp, copy))
    waits = []
    for layer, ds, index, grp, copy in relays:
        waits.append(copy)
        for dg in range(1, groups):
            grp[dg].wait_recv()
            there = view(layer, lax.rem(g - dg + groups, groups), r, index)
            relay = send(
                there,
                there,
                core_send.at[ds - 1, dg, index],
                core_recv.at[ds - 1, dg, index],
                other_row,
            )
            relay.start()
            waits.append(relay)
    for copy in waits:
        copy.wait_recv()

    for step_no in range(STEPS):
        if step_no:
            hidden = encoded(state, step_no)
        for layer in range(segments):
            spacing = 2 ** (layer % 3)
            wide = hidden.astype(jnp.float32)
            for row in range(rows):
                here = wide[:, row * lon : (row + 1) * lon]
                for at, offset in enumerate((-spacing, 0, spacing)):
                    taps[at * channels : (at + 1) * channels, row * lon : (row + 1) * lon] = shifted(
                        here, offset
                    ).astype(jnp.bfloat16)
            span = 3 * channels
            conv = jnp.dot(
                conv_all[layer, :, span : 2 * span], taps[...], preferred_element_type=jnp.float32
            )
            below = jnp.dot(
                conv_all[layer, :, 2 * span :], taps[:, lon:], preferred_element_type=jnp.float32
            )
            above = jnp.dot(
                conv_all[layer, :, :span], taps[:, :lon], preferred_element_type=jnp.float32
            )
            conv = conv + jnp.concatenate([below, above], axis=1)
            centred = conv - jnp.mean(conv, axis=0, keepdims=True)
            spread = jnp.mean(centred * centred, axis=0, keepdims=True)
            gain = to_column(gain_all[layer].astype(jnp.float32))
            normed = centred * lax.rsqrt(spread + 1e-05) * gain
            activated = jax.nn.gelu(normed).astype(jnp.bfloat16)
            mixed = jnp.dot(point_all[layer], activated, preferred_element_type=jnp.float32)
            hidden = (land * (wide + mixed)).astype(jnp.bfloat16)
        change = jnp.dot(decode_weight, hidden, preferred_element_type=jnp.float32)
        state = (state + land * change).astype(jnp.bfloat16).astype(jnp.float32)

    own_final = jnp.where(head, state[:, :lon], state[:, lon:])
    final_ref[0, 0, 0] = own_final.astype(jnp.bfloat16)
    mean_copies = []
    for dm in range(1, members):
        copy = send(
            final_ref.at[0, 0, 0],
            final_all.at[m],
            mean_send.at[dm - 1],
            mean_recv.at[dm - 1],
            device(dm=dm),
        )
        copy.start()
        mean_copies.append(copy)
    final_all[m] = own_final.astype(jnp.bfloat16)
    for copy in seg_copies.values():
        copy.wait_send()
    for layer, ds, index, grp, copy in relays:
        for dg in range(1, groups):
            grp[dg].wait_send()
    for copy in waits:
        copy.wait_send()
    for copy in mean_copies:
        copy.wait()
    total = jnp.zeros(own_final.shape, jnp.float32)
    for member in range(members):
        total = total + final_all[member].astype(jnp.float32)
    mean_ref[0, 0] = total / members


def solution(mesh):
    sizes = tuple(mesh.shape[axis] for axis in ("groups", "members", "segment", "rows"))
    groups, members, segments, rows = sizes

    def per_device(*args):
        init, slots, conv = args[0], args[1], args[9]
        variables, lon = init.shape[2:]
        forces = slots.shape[4]
        channels = conv.shape[1]
        vmem = pl.BlockSpec(memory_space=pltpu.VMEM)
        hbm = pl.BlockSpec(memory_space=pltpu.HBM)
        args = list(args)
        args[5] = args[5].T
        args[8] = args[8].T
        dma = pltpu.SemaphoreType.DMA
        pieces = CONV_CHUNKS + 1
        mates = members * rows - 1
        away = max(segments - 1, 1)
        local = [
            pltpu.SMEM(args[i].shape, args[i].dtype) if i in (2, 4) else pltpu.VMEM(args[i].shape, args[i].dtype)
            for i in (0, 2, 3, 4, 5, 6, 7, 8, 12)
        ]
        scratch = local + [
            pltpu.VMEM((segments,) + conv.shape[1:], jnp.bfloat16),
            pltpu.VMEM((segments, channels, channels), jnp.bfloat16),
            pltpu.VMEM((segments, 1, channels), jnp.bfloat16),
            pltpu.VMEM((variables, lon), jnp.bfloat16),
            pltpu.VMEM((1, lon), jnp.int32),
            pltpu.VMEM((members, rows, STEPS, forces, lon), jnp.bfloat16),
            pltpu.VMEM((members, variables, lon), jnp.bfloat16),
            pltpu.VMEM((-(-(variables + forces) // 8) * 8, rows * lon), jnp.float32),
            pltpu.VMEM((3 * channels, rows * lon), jnp.bfloat16),
            dma((2,)),
            dma((2,)),
            dma((mates,)),
            dma((mates,)),
            dma((away, pieces)),
            dma((away, pieces)),
            dma((away, max(groups - 1, 1), pieces)),
            dma((away, max(groups - 1, 1), pieces)),
            dma((away, groups, pieces)),
            dma((away, groups, pieces)),
            dma((away,)),
            dma((away,)),
            dma((max(members - 1, 1),)),
            dma((max(members - 1, 1),)),
            dma((13,)),
        ]
        return pl.pallas_call(
            functools.partial(kernel, sizes),
            out_shape=(
                jax.ShapeDtypeStruct((1, 1, 1, variables, lon), jnp.bfloat16),
                jax.ShapeDtypeStruct((1, 1, variables, lon), jnp.float32),
            ),
            in_specs=[hbm] * 13,
            out_specs=(vmem, vmem),
            scratch_shapes=scratch,
            compiler_params=pltpu.CompilerParams(
                collective_id=0, has_side_effects=True
            ),
        )(*args)

    in_specs = (
        P(("groups", "segment"), "rows", None, None),
        P("members", ("groups", "segment"), None, "rows", None, None),
        P(("groups", "segment"), None),
        P(("groups", "rows"), None),
        P(("groups", "members")),
        P(),
        P(),
        P(),
        P(),
        P("segment", None, None),
        P("segment", None, None),
        P("segment", None),
        P(),
    )
    out_specs = (
        P("members", ("groups", "segment"), "rows", None, None),
        P(("groups", "segment"), "rows", None, None),
    )
    return jax.shard_map(
        per_device, mesh=mesh, in_specs=in_specs, out_specs=out_specs, check_vma=False
    )
```
